512 devices in a mesh: graphs: 8 (over x, y_hi), dom: 64 (over y_lo, z, core).
Axes of the slice: x: 4, y: 8 (y_hi: 2, y_lo: 4; y = y_hi * 4 + y_lo), z: 8, core: 2. Of those that a mesh axis runs over, the one named last changes fastest.
Arguments:
- node_feats: float32 [65536, 256], P(('graphs', 'dom')), parts along dimension 0, may hold values from -6 to 6
- norm_gain: float32 [256], replicated, may hold values from 0.1 to 1.9
- w_query: bfloat16 [256, 256], replicated, may hold values from -32 to 32
- w_key: bfloat16 [256, 256], replicated, may hold values from -1 to 1
- w_value: bfloat16 [256, 256], replicated, may hold values from -0.375 to 0.375
- w_out: bfloat16 [256, 256], replicated, may hold values from -0.75 to 0.75
- msg_src_w: bfloat16 [256, 256], replicated, may hold values from -0.25 to 0.25
- msg_dst_w: bfloat16 [256, 256], replicated, may hold values from -0.25 to 0.25
- msg_bias: float32 [256], replicated, may hold values from -4 to 4
- msg_out_w: bfloat16 [256, 256], replicated, may hold values from -0.25 to 0.25
- msg_out_bias: float32 [256], replicated, may hold values from -3 to 3
- mlp_gain: float32 [256], replicated, may hold values from 0.1 to 1.9
- mlp_up: bfloat16 [256, 1024], replicated, may hold values from -0.375 to 0.375
- mlp_down: bfloat16 [1024, 256], replicated, may hold values from -0.1875 to 0.1875
- send_list: int32 [512, 64, 4], P(('graphs', 'dom')), parts along dimension 0, may hold values from 0 to 127
- send_count: int32 [512, 64], P('graphs', 'dom'), parts along dimension 0, may hold values from 0 to 4, as said below
- edge_src: int32 [512, 8, 128], P(('graphs', 'dom')), parts along dimension 0, may hold values from 0 to 383
- edge_dst: int32 [512, 8, 128], P(('graphs', 'dom')), parts along dimension 0, may hold values from 0 to 127
- edge_count: int32 [512], P(('graphs', 'dom')), parts along dimension 0, may hold values from 256 to 1024, as said below
Outputs:
- out_feats: float32 [65536, 256], P(('graphs', 'dom')), parts along dimension 0
The draws below stay inside these ranges and needn't reach their ends.
There are 8 independent parts, one for each index of `graphs`. The reference program is written for one: setup_inputs(seed, part) draws one part's arguments, and reference() takes and returns one part's arrays. A program takes and returns all parts, laid end to end along the dimension named above; an argument that names none is the same for every part. Nothing has to cross between parts.
Inputs may be any that keep to these rules, and one draw needn't show every extreme that they name: `send_list`: entries in slots at or past the count are arbitrary local rows. `send_count`: some sender fills all 4 slots to some receiver. `edge_src`: slots below 128 are local nodes; slot 128 + p * 4 + j is slot j of the rows received from partition p. `edge_count`: live edge slots come first in a partition's order; some partition has all 1024 slots live.
All inputs are finite; a program needn't handle non-finite values.
Results may differ from the reference program's by a relative error of at most 0.0057.
Values may be sent and summed in bfloat16 or wider, within the bound.
No kernel may reach another device: no remote copies, remote signals or barrier semaphores. Data moves between devices by JAX's collectives and lax.ppermute only.
A program may use at most 64 MiB of HBM per device.

```python
import math
import jax
import jax.numpy as jnp
from jax import lax

D = 256
HEADS = 8
FF = 1024
NODE_DEV = 128
BMAX = 4
ETILES = 8
EDGE_TILE = 128
NODES = 8192
N_DOM = 64


def paired_weights(key):
    base_key = jax.random.fold_in(key, 7001)
    first_key, second_key, third_key = jax.random.split(base_key, 3)
    factor = D ** (-0.5)
    key_weights = jax.random.truncated_normal(first_key, -4.0, 4.0, (D, D), jnp.float32) * factor
    head_spread = jnp.exp(jax.random.uniform(third_key, (HEADS,), jnp.float32, math.log(2.4), math.log(3.2)))
    spread_columns = jnp.repeat(head_spread, D // HEADS)
    random_query = jax.random.truncated_normal(second_key, -4.0, 4.0, (D, D), jnp.float32) * factor * spread_columns[None, :]
    query_weights = random_query
    return (query_weights, key_weights)


def draw_w_query(key, part):
    return paired_weights(key)[0].astype(jnp.bfloat16)


def draw_w_key(key, part):
    return paired_weights(key)[1].astype(jnp.bfloat16)


def draw_send_count(key, part):
    base_key = jax.random.fold_in(key, 7101)
    first_key, second_key = jax.random.split(base_key)
    counts = jax.random.randint(first_key, (N_DOM * N_DOM,), 0, BMAX + 1)
    chosen = jax.random.randint(second_key, (), 0, N_DOM * N_DOM)
    counts = jnp.where(jnp.arange(N_DOM * N_DOM) == chosen, BMAX, counts)
    return counts.reshape(N_DOM, N_DOM).astype(jnp.int32)


def draw_edge_count(key, part):
    base_key = jax.random.fold_in(key, 7201)
    first_key, second_key = jax.random.split(base_key)
    capacity = ETILES * EDGE_TILE
    counts = jax.random.randint(first_key, (N_DOM,), capacity // 4, capacity + 1)
    chosen = jax.random.randint(second_key, (), 0, N_DOM)
    counts = jnp.where(jnp.arange(N_DOM) == chosen, capacity, counts)
    return counts.astype(jnp.int32)


def plant(drawn, own_key, low, top_value):
    longest = drawn.shape.index(max(drawn.shape))
    spots = []
    for shift in (0, 1):
        where = [jax.random.randint(jax.random.fold_in(own_key, axis), (), 0, length) for axis, length in enumerate(drawn.shape)]
        where[longest] = (where[longest] + shift) % drawn.shape[longest]
        spots.append(tuple(where))
    return drawn.at[spots[0]].set(low).at[spots[1]].set(top_value)


def block_scale(stream_key, shape, cuts, low, high):
    level = 1.0
    for axis_at, parts in cuts:
        steps = jax.random.uniform(jax.random.fold_in(jax.random.fold_in(stream_key, 6), axis_at), (parts,), jnp.float32, low / len(cuts), high / len(cuts))
        level = level * jnp.repeat(jnp.exp(steps), shape[axis_at] // parts).reshape((-1,) + (1,) * (len(shape) - 1 - axis_at))
    return level


def bell_draw(key, shape, scale, most, pieces=(), held_as=jnp.bfloat16):
    array = scale * jax.random.normal(key, shape, jnp.float32)
    if pieces:
        array = array * block_scale(key, shape, pieces, -0.22, 0.18)
    return jnp.clip(array, -most, most).astype(held_as)


def setup_inputs(seed: int = 0, part: int = 0) -> dict:
    streams_of = jax.random.split(jax.random.key(seed), 20)
    part_splits = jax.random.split(jax.random.fold_in(streams_of[19], part), 20)
    return {
        "node_feats": bell_draw(part_splits[0], (NODES, D), 1.0, 6.0, ((0, 64),), jnp.float32),
        "norm_gain": jnp.clip(1.0 + 0.18 * jax.random.normal(streams_of[1], (D,), jnp.float32), 0.1, 1.9),
        "w_query": draw_w_query(jax.random.fold_in(streams_of[19], 71), part),
        "w_key": draw_w_key(jax.random.fold_in(streams_of[19], 71), part),
        "w_value": bell_draw(streams_of[4], (D, D), D ** -0.5, 0.375),
        "w_out": bell_draw(streams_of[5], (D, D), (D // 4) ** -0.5, 0.75),
        "msg_src_w": bell_draw(streams_of[6], (D, D), (2 * D) ** -0.5, 0.25),
        "msg_dst_w": bell_draw(streams_of[7], (D, D), (2 * D) ** -0.5, 0.25),
        "msg_bias": bell_draw(streams_of[8], (D,), 1.0, 4.0, (), jnp.float32),
        "msg_out_w": bell_draw(streams_of[9], (D, D), (2 * D) ** -0.5, 0.25),
        "msg_out_bias": bell_draw(streams_of[10], (D,), 0.5, 3.0, (), jnp.float32),
        "mlp_gain": jnp.clip(1.0 + 0.18 * jax.random.normal(streams_of[11], (D,), jnp.float32), 0.1, 1.9),
        "mlp_up": bell_draw(streams_of[12], (D, FF), D ** -0.5, 0.375),
        "mlp_down": bell_draw(streams_of[13], (FF, D), FF ** -0.5, 0.1875),
        "send_list": plant(jax.random.randint(part_splits[14], (N_DOM, N_DOM, BMAX), 0, NODE_DEV), jax.random.fold_in(part_splits[14], 1), 0, NODE_DEV - 1).astype(jnp.int32),
        "send_count": draw_send_count(jax.random.fold_in(jax.random.fold_in(streams_of[19], part), 71), part),
        "edge_src": plant(jax.random.randint(part_splits[16], (N_DOM, ETILES, EDGE_TILE), 0, NODE_DEV + N_DOM * BMAX), jax.random.fold_in(part_splits[16], 1), 0, (NODE_DEV + N_DOM * BMAX) - 1).astype(jnp.int32),
        "edge_dst": plant(jax.random.randint(part_splits[17], (N_DOM, ETILES, EDGE_TILE), 0, NODE_DEV), jax.random.fold_in(part_splits[17], 1), 0, NODE_DEV - 1).astype(jnp.int32),
        "edge_count": draw_edge_count(jax.random.fold_in(jax.random.fold_in(streams_of[19], part), 71), part),
    }


def rms_norm(features, scale_gain):
    return features * lax.rsqrt(lax.optimization_barrier(jnp.mean(features * features, axis=-1, keepdims=True)) + 1e-06) * scale_gain.astype(jnp.float32)

def reference(node_feats, norm_gain, w_query, w_key, w_value, w_out, msg_src_w, msg_dst_w, msg_bias, msg_out_w, msg_out_bias, mlp_gain, mlp_up, mlp_down, send_list, send_count, edge_src, edge_dst, edge_count):
    head_size = D // HEADS
    normed = rms_norm(node_feats, norm_gain).astype(jnp.bfloat16)
    queries = jnp.dot(normed, w_query, preferred_element_type=jnp.float32).astype(jnp.bfloat16)
    keys = jnp.dot(normed, w_key, preferred_element_type=jnp.float32).astype(jnp.bfloat16)
    values = jnp.dot(normed, w_value, preferred_element_type=jnp.float32).astype(jnp.bfloat16)
    key_heads = keys.reshape(NODES, HEADS, head_size).astype(jnp.float32)
    value_heads = values.reshape(NODES, HEADS, head_size).astype(jnp.float32)
    query_blocks = queries.reshape(N_DOM, NODE_DEV, HEADS, head_size)

    def attend(query_block):
        scores = jnp.einsum('qhd,khd->hqk', query_block.astype(jnp.float32), key_heads) * head_size ** (-0.5)
        row_max = lax.optimization_barrier(jnp.max(scores, axis=-1, keepdims=True))
        weights = jnp.exp(scores - row_max)
        totals = lax.optimization_barrier(jnp.sum(weights, axis=-1))
        probs = lax.optimization_barrier(weights.astype(jnp.bfloat16)).astype(jnp.float32)
        mixed = jnp.einsum('hqk,khd->qhd', probs, value_heads)
        return (mixed / jnp.transpose(totals)[:, :, None]).astype(jnp.bfloat16)
    attended = lax.map(attend, query_blocks).reshape(NODES, D)
    global_part = jnp.dot(attended, w_out, preferred_element_type=jnp.float32)
    device_ids = jnp.arange(N_DOM, dtype=jnp.int32)[:, None, None]
    is_local = edge_src < NODE_DEV
    slot_index = jnp.maximum(edge_src - NODE_DEV, 0).astype(jnp.int32)
    sender = (slot_index // BMAX).astype(jnp.int32)
    lane_slot = (slot_index % BMAX).astype(jnp.int32)
    device_full = jnp.broadcast_to(device_ids, edge_src.shape)
    remote_row = send_list[sender, device_full, lane_slot]
    source = jnp.where(is_local, device_full * NODE_DEV + edge_src, sender * NODE_DEV + remote_row).astype(jnp.int32)
    slot_live = is_local | (lane_slot < send_count[sender, device_full])
    positions = jnp.arange(ETILES, dtype=jnp.int32)[:, None] * EDGE_TILE + jnp.arange(EDGE_TILE, dtype=jnp.int32)[None, :]
    edge_live = slot_live & (positions[None, :, :] < edge_count[:, None, None])
    destination = (device_full * NODE_DEV + edge_dst).astype(jnp.int32).reshape(-1)
    src_feats = normed[source.reshape(-1)]
    dst_feats = normed[destination]
    pre_act = jnp.dot(src_feats, msg_src_w, preferred_element_type=jnp.float32) + jnp.dot(dst_feats, msg_dst_w, preferred_element_type=jnp.float32) + msg_bias.astype(jnp.float32)
    hidden = jax.nn.silu(pre_act).astype(jnp.bfloat16)
    message = (jnp.dot(hidden, msg_out_w, preferred_element_type=jnp.float32) + msg_out_bias.astype(jnp.float32)).astype(jnp.bfloat16)
    message = jnp.where(edge_live.reshape(-1)[:, None], message.astype(jnp.float32), jnp.zeros((), jnp.float32))
    local_part = jax.ops.segment_sum(message, destination, num_segments=NODES)
    mid = node_feats + local_part + global_part
    mid_normed = rms_norm(mid, mlp_gain).astype(jnp.bfloat16)
    lifted = jax.nn.gelu(jnp.dot(mid_normed, mlp_up, preferred_element_type=jnp.float32)).astype(jnp.bfloat16)
    return mid + jnp.dot(lifted, mlp_down, preferred_element_type=jnp.float32)
```

```python
import functools
import math

import jax
import jax.numpy as jnp
from jax import lax
from jax.experimental import pallas as pl
from jax.experimental.pallas import tpu as pltpu
from jax.sharding import Mesh
from jax.sharding import PartitionSpec as P

HEADS = 8
NODES = 128
WIDTH = 256
HEAD = WIDTH // HEADS
SLOTS = 4
DOMS = 64
DOM = ("ya", "yb", "za", "zb", "core")
GRAPHS_DOM = ("graphs",) + DOM
HEAD_AXES = ("ya", "za")
CHIP_AXES = ("yb", "zb")
CHIPS = 4
F32 = jnp.float32
BF16 = jnp.bfloat16
SCALE = math.log2(math.e) / math.sqrt(HEAD)
VM = pl.BlockSpec(memory_space=pltpu.VMEM)
SM = pl.BlockSpec(memory_space=pltpu.SMEM)
KV_ROWS = 8 * 2 * HEAD
SENT_ROWS = KV_ROWS + 8 * 16


def iota(shape, dim):
    return lax.broadcasted_iota(jnp.int32, shape, dim)


def mm(a, b, dims=((1,), (0,))):
    return lax.dot_general(a, b, (dims, ((), ())), preferred_element_type=F32)


def rms(x, gain):
    return x * lax.rsqrt(jnp.mean(x * x, axis=-1, keepdims=True) + 1e-06) * gain


def project_kernel(feats, gain, wq, wk, wv, lists, normed_out, sent):
    normed = rms(feats[...], gain[...]).astype(BF16)
    normed_out[...] = normed
    for first, weight, factor in ((0, wq, SCALE), (HEAD, wk, None), (2 * HEAD, wv, None)):
        out = mm(normed, weight[...])
        if factor is not None:
            out = out * factor
        turned = out.T.astype(BF16)
        for h in range(HEADS):
            sent[h, first : first + HEAD, :] = turned[h * HEAD : (h + 1) * HEAD, :]
    place = iota((DOMS * SLOTS, DOMS), 0)
    receiver = (
        ((place >> 7) & 1) * 32
        + ((place >> 4) & 1) * 16
        + ((place >> 5) & 3) * 4
        + ((place >> 2) & 3)
    )
    pick_receiver = (receiver == iota((DOMS * SLOTS, DOMS), 1)).astype(BF16)
    spread = mm(pick_receiver, lists[0].astype(F32).astype(BF16), ((1,), (1,)))
    own_slot = (iota(spread.shape, 0) & 3) == iota(spread.shape, 1)
    index = jnp.sum(jnp.where(own_slot, spread, 0.0), axis=1, keepdims=True)
    lanes = iota((DOMS * SLOTS, NODES), 1).astype(F32)
    rows = mm((lanes == index).astype(BF16), normed)
    for h in range(HEADS):
        parts = []
        for chip in range(CHIPS):
            at = h * 32 + chip * 8
            parts += [rows[at : at + 8, :128], rows[at : at + 8, 128:]]
        sent[h, 3 * HEAD :, :] = jnp.concatenate(parts, axis=0).astype(BF16)


def repack_kernel(got, sent):
    for chip in range(CHIPS):
        for s in range(8):
            sent[chip, s * 64 : (s + 1) * 64, :] = got[s, HEAD : 3 * HEAD, :]
            sent[chip, KV_ROWS + s * 16 : KV_ROWS + (s + 1) * 16, :] = got[
                s, 96 + chip * 16 : 112 + chip * 16, :
            ]


KEYS = CHIPS * 8 * NODES
QUERIES = 8 * NODES
Q_BLOCK = 256


def load_operands(got, kv, q_s, k_s, v_s):
    for s in range(8):
        q_s[s * 128 : (s + 1) * 128, :] = got[s, 0:HEAD, :].T
    for chip in range(CHIPS):
        for s in range(8):
            at = (chip * 8 + s) * 128
            k_s[:, at : at + 128] = kv[chip, s * 64 : s * 64 + 32, :]
            v_s[0:32, at : at + 128] = kv[chip, s * 64 + 32 : s * 64 + 64, :]
    v_s[32:64, :] = jnp.ones((32, KEYS), BF16)


def attend_first_kernel(got, kv, acc_out, max_out, q_s, k_s, v_s):
    load_operands(got, kv, q_s, k_s, v_s)
    for b in range(QUERIES // Q_BLOCK):
        at = slice(b * Q_BLOCK, (b + 1) * Q_BLOCK)
        scores = mm(q_s[at, :], k_s[...])
        top = jnp.max(scores, axis=1, keepdims=True)
        weights = jnp.exp2(scores - top).astype(BF16)
        acc_out[at, :] = mm(weights, v_s[...], ((1,), (1,)))
        max_out[at, :] = jnp.broadcast_to(top, (Q_BLOCK, 128))


def attend_last_kernel(got, kv, acc_in, max_in, out, q_s, k_s, v_s):
    load_operands(got, kv, q_s, k_s, v_s)
    for b in range(QUERIES // Q_BLOCK):
        at = slice(b * Q_BLOCK, (b + 1) * Q_BLOCK)
        scores = mm(q_s[at, :], k_s[...])
        before = max_in[at, 0:1]
        top = jnp.maximum(before, jnp.max(scores, axis=1, keepdims=True))
        weights = jnp.exp2(scores - top).astype(BF16)
        acc = acc_in[at, :] * jnp.exp2(before - top) + mm(weights, v_s[...], ((1,), (1,)))
        done = (acc[:, 0:32] / acc[:, 32:33]).T.astype(BF16)
        for i in range(Q_BLOCK // 128):
            out[b * (Q_BLOCK // 128) + i] = done[:, i * 128 : (i + 1) * 128]


def edge_kernel(
    limit, place, normed, mine, other, counts, src, dst, w_src, w_dst, b1, w_out, b2, feats, out
):
    edges = src.shape[1] * src.shape[2]
    tiles = src.shape[1]
    row = lambda ref: jnp.concatenate([ref[0, t : t + 1, :] for t in range(tiles)], axis=1)
    src_row, dst_row = row(src), row(dst)
    core = place[0]
    table = [normed[...].astype(F32)]
    for part in (mine, other):
        for chip in range(CHIPS):
            for s in range(8):
                pair = part[chip, KV_ROWS + s * 16 : KV_ROWS + (s + 1) * 16, :].astype(F32)
                table.append(jnp.concatenate([pair[:8], pair[8:]], axis=1))
    table = jnp.concatenate(table, axis=0).astype(BF16)
    total = 512
    at = iota((total, 1), 0)
    sender_core = jnp.where(at >= 256, 1 - core, core)
    chip, s, to, slot = (at >> 6) & 3, (at >> 3) & 7, (at >> 2) & 1, at & 3
    sender = (
        (s >> 2) * 32 + (chip >> 1) * 16 + (s & 3) * 4 + (chip & 1) * 2 + sender_core
    )
    wide = iota((total, DOMS), 1)
    held = jnp.broadcast_to(counts[...].astype(F32), (8, DOMS)).astype(BF16)
    count = mm((sender == wide).astype(BF16), held, ((1,), (1,)))[:, 0:1]
    live_slot = (to == core) & (slot.astype(F32) < count)
    ids = jnp.where(live_slot, NODES + sender * SLOTS + slot, -1)
    ids = jnp.concatenate([iota((NODES, 1), 0), ids], axis=0)
    pick = (ids == src_row).astype(F32).astype(BF16)
    to_node = iota((NODES, 1), 0) == dst_row
    pick_dst = to_node.astype(F32).astype(BF16)
    hit = mm(jnp.ones((8, ids.shape[0]), BF16), pick)[0:1, :]
    live = jnp.where(iota((1, edges), 1) < limit[0], hit, 0.0)
    src_feats = mm(table, pick, ((0,), (0,))).astype(BF16)
    dst_feats = mm(normed[...], pick_dst, ((0,), (0,))).astype(BF16)
    column = lambda ref: jnp.broadcast_to(ref[...], (8, WIDTH)).T[:, 0:1]
    pre = (
        mm(w_src[...], src_feats, ((0,), (0,)))
        + mm(w_dst[...], dst_feats, ((0,), (0,)))
        + column(b1)
    )
    hidden = jax.nn.silu(pre).astype(BF16)
    message = (mm(w_out[...], hidden, ((0,), (0,))) + column(b2)).astype(BF16)
    spread = jnp.where(to_node, live, 0.0).astype(BF16)
    out[...] = feats[...] + mm(spread, message, ((1,), (1,)))


def finish_kernel(base, attended, w_out, gain, up, down, out):
    turned = jnp.concatenate([attended[h] for h in range(HEADS)], axis=0)
    mid = base[...] + mm(turned, w_out[...], ((0,), (0,)))
    lifted = jax.nn.gelu(mm(rms(mid, gain[...]).astype(BF16), up[...])).astype(BF16)
    out[...] = mid + mm(lifted, down[...])


def body(
    node_feats,
    norm_gain,
    w_query,
    w_key,
    w_value,
    w_out,
    msg_src_w,
    msg_dst_w,
    msg_bias,
    msg_out_w,
    msg_out_bias,
    mlp_gain,
    mlp_up,
    mlp_down,
    send_list,
    send_count,
    edge_src,
    edge_dst,
    edge_count,
):
    shape = jax.ShapeDtypeStruct
    row = lambda v: v.reshape(1, WIDTH)
    normed, sent = pl.pallas_call(
        project_kernel,
        out_shape=(shape((NODES, WIDTH), BF16), shape((HEADS, 160, 128), BF16)),
        in_specs=[VM] * 6,
        out_specs=(VM, VM),
        name="project",
    )(node_feats, row(norm_gain), w_query, w_key, w_value, jnp.swapaxes(send_list, 1, 2))
    got = lax.all_to_all(sent, HEAD_AXES, 0, 0, tiled=True)
    shared = pl.pallas_call(
        repack_kernel,
        out_shape=shape((CHIPS, SENT_ROWS, 128), BF16),
        in_specs=[VM],
        out_specs=VM,
        name="repack",
    )(got)
    mine = lax.all_to_all(shared, CHIP_AXES, 0, 0, tiled=True)
    other = lax.ppermute(mine, "core", [(0, 1), (1, 0)])
    scratch = [
        pltpu.VMEM((QUERIES, HEAD), BF16),
        pltpu.VMEM((HEAD, KEYS), BF16),
        pltpu.VMEM((2 * HEAD, KEYS), BF16),
    ]
    acc, top = pl.pallas_call(
        attend_first_kernel,
        out_shape=(shape((QUERIES, 64), F32), shape((QUERIES, 128), F32)),
        in_specs=[VM] * 2,
        out_specs=(VM, VM),
        scratch_shapes=scratch,
        name="attend_first",
    )(got, mine)
    attended = pl.pallas_call(
        attend_last_kernel,
        out_shape=shape((8, HEAD, NODES), BF16),
        in_specs=[VM] * 4,
        out_specs=VM,
        scratch_shapes=scratch,
        name="attend_last",
    )(got, other, acc, top)
    back = lax.all_to_all(attended, HEAD_AXES, 0, 0, tiled=True)
    core = lax.axis_index("core").reshape(1).astype(jnp.int32)
    base = pl.pallas_call(
        edge_kernel,
        out_shape=shape((NODES, WIDTH), F32),
        in_specs=[SM, SM] + [VM] * 12,
        out_specs=VM,
        name="edges",
    )(
        edge_count,
        core,
        normed,
        mine,
        other,
        send_count.T,
        edge_src,
        edge_dst,
        msg_src_w,
        msg_dst_w,
        row(msg_bias),
        msg_out_w,
        row(msg_out_bias),
        node_feats,
    )
    return pl.pallas_call(
        finish_kernel,
        out_shape=shape((NODES, WIDTH), F32),
        in_specs=[VM] * 6,
        out_specs=VM,
        name="finish",
    )(base, back, w_out, row(mlp_gain), mlp_up, mlp_down)


def solution(mesh):
    finer = Mesh(
        mesh.devices.reshape(mesh.shape["graphs"], 2, 2, 4, 2, 2), ("graphs",) + DOM
    )
    rows = P(GRAPHS_DOM, None)
    blocks = P(GRAPHS_DOM, None, None)
    placed = (rows,) + (P(),) * 13 + (blocks, P("graphs", DOM), blocks, blocks, P(GRAPHS_DOM))
    return jax.shard_map(body, mesh=finer, in_specs=placed, out_specs=rows, check_vma=False)
```

```python
import math

import jax
import jax.numpy as jnp
from jax import lax
from jax.experimental import pallas as pl
from jax.experimental.pallas import tpu as pltpu
from jax.sharding import Mesh
from jax.sharding import PartitionSpec as P


HEADS = 8
NODES = 128
WIDTH = 256
HEAD = WIDTH // HEADS
SLOTS = 4
DOMS = 64
DOM = ("ya", "yb", "za", "zb", "core")
GRAPHS_DOM = ("graphs",) + DOM
HEAD_AXES = ("ya", "za")
CHIP_AXES = ("yb", "zb")
CHIPS = 4
F32 = jnp.float32
BF16 = jnp.bfloat16
SCALE = math.log2(math.e) / math.sqrt(HEAD)
VM = pl.BlockSpec(memory_space=pltpu.VMEM)
SM = pl.BlockSpec(memory_space=pltpu.SMEM)
KV = 2 * HEAD
KV_ROWS = 8 * KV
SENT_ROWS = KV_ROWS + 8 * 16
RING = 8 * NODES
Q_BLOCK = 256
TOP_LANE = 48
ROOM = pltpu.CompilerParams(vmem_limit_bytes=28 * 2**20)


def iota(shape, dim):
    return lax.broadcasted_iota(jnp.int32, shape, dim)


def mm(a, b, dims=((1,), (0,))):
    return lax.dot_general(a, b, (dims, ((), ())), preferred_element_type=F32)


def rms(x, gain):
    return x * lax.rsqrt(jnp.mean(x * x, axis=-1, keepdims=True) + 1e-06) * gain


def project_kernel(feats, gain, wq, wk, wv, lists, normed_out, sent):
    normed = rms(feats[...], gain[...]).astype(BF16)
    normed_out[...] = normed
    for first, weight, factor in ((0, wq, SCALE), (HEAD, wk, None), (2 * HEAD, wv, None)):
        out = mm(normed, weight[...])
        if factor is not None:
            out = out * factor
        turned = out.T.astype(BF16)
        for h in range(HEADS):
            sent[h, first : first + HEAD, :] = turned[h * HEAD : (h + 1) * HEAD, :]
    place = iota((DOMS * SLOTS, DOMS), 0)
    receiver = (
        ((place >> 7) & 1) * 32
        + ((place >> 4) & 1) * 16
        + ((place >> 5) & 3) * 4
        + ((place >> 2) & 3)
    )
    pick_receiver = (receiver == iota((DOMS * SLOTS, DOMS), 1)).astype(BF16)
    spread = mm(pick_receiver, lists[0].astype(F32).astype(BF16), ((1,), (1,)))
    own_slot = (iota(spread.shape, 0) & 3) == iota(spread.shape, 1)
    index = jnp.sum(jnp.where(own_slot, spread, 0.0), axis=1, keepdims=True)
    lanes = iota((DOMS * SLOTS, NODES), 1).astype(F32)
    rows = mm((lanes == index).astype(BF16), normed)
    for h in range(HEADS):
        parts = []
        for chip in range(CHIPS):
            at = h * 32 + chip * 8
            parts += [rows[at : at + 8, :128], rows[at : at + 8, 128:]]
        sent[h, 3 * HEAD :, :] = jnp.concatenate(parts, axis=0).astype(BF16)


def repack_kernel(got, sent, own):
    for s in range(8):
        own[s] = got[s, HEAD : 3 * HEAD, :]
    for chip in range(CHIPS):
        for s in range(8):
            sent[chip, s * 64 : (s + 1) * 64, :] = got[s, HEAD : 3 * HEAD, :]
            sent[chip, KV_ROWS + s * 16 : KV_ROWS + (s + 1) * 16, :] = got[
                s, 96 + chip * 16 : 112 + chip * 16, :
            ]


def load_queries(got, q_s):
    for s in range(8):
        q_s[s * 128 : (s + 1) * 128, :] = got[s, 0:HEAD, :].T


def load_keys(pieces, k_s, v_s):
    for at, piece in enumerate(pieces):
        lanes = slice(at * 128, (at + 1) * 128)
        k_s[:, lanes] = piece[:HEAD, :]
        v_s[0:HEAD, lanes] = piece[HEAD:, :]
    v_s[HEAD:, :] = jnp.ones((HEAD, v_s.shape[1]), BF16)


def attend(q_s, k_s, v_s, before, after):
    def scores_of(b):
        return mm(q_s[b * Q_BLOCK : (b + 1) * Q_BLOCK, :], k_s[...])

    blocks = RING // Q_BLOCK
    scores = scores_of(0)
    for b in range(blocks):
        upcoming = scores_of(b + 1) if b + 1 < blocks else None
        at = slice(b * Q_BLOCK, (b + 1) * Q_BLOCK)
        top = jnp.max(scores, axis=1, keepdims=True)
        if before is not None:
            old = before[at, TOP_LANE : TOP_LANE + 1]
            top = jnp.maximum(old, top)
        weights = jnp.exp2(scores - top).astype(BF16)
        acc = mm(weights, v_s[...], ((1,), (1,)))
        if before is not None:
            acc = acc + before[at, :] * jnp.exp2(old - top)
        after(b, at, acc, top)
        scores = upcoming


def keep(state_out):
    def after(b, at, acc, top):
        state_out[at, :] = jnp.where(iota(acc.shape, 1) < TOP_LANE, acc, top)

    return after


def attend_own_kernel(got, partner, state, q_s, k_s, v_s):
    load_queries(got, q_s)
    pieces = [got[s, HEAD : 3 * HEAD, :] for s in range(8)]
    load_keys(pieces + [partner[s] for s in range(8)], k_s, v_s)
    attend(q_s, k_s, v_s, None, keep(state))


def load_near(place, got, kv, q_s, k_s, v_s):
    load_queries(got, q_s)
    pieces = []
    for turn in range(1, CHIPS):
        chip = (place[0] + turn) & (CHIPS - 1)
        pieces += [kv[chip, s * KV : (s + 1) * KV, :] for s in range(8)]
    load_keys(pieces, k_s, v_s)


def attend_near_kernel(place, got, kv, before, state, q_s, k_s, v_s):
    load_near(place, got, kv, q_s, k_s, v_s)
    attend(q_s, k_s, v_s, before, keep(state))


def attend_last_kernel(place, got, kv, before, out, q_s, k_s, v_s):
    load_near(place, got, kv, q_s, k_s, v_s)

    def after(b, at, acc, top):
        done = (acc[:, :HEAD] / acc[:, HEAD : HEAD + 1]).T.astype(BF16)
        for i in range(Q_BLOCK // 128):
            out[b * (Q_BLOCK // 128) + i] = done[:, i * 128 : (i + 1) * 128]

    attend(q_s, k_s, v_s, before, after)


def edge_kernel(
    limit, place, normed, mine, other, counts, src, dst, w_src, w_dst, b1, w_out, b2, feats, out
):
    edges = src.shape[1] * src.shape[2]
    tiles = src.shape[1]
    row = lambda ref: jnp.concatenate([ref[0, t : t + 1, :] for t in range(tiles)], axis=1)
    src_row, dst_row = row(src), row(dst)
    core = place[0]
    table = [normed[...].astype(F32)]
    for part in (mine, other):
        for chip in range(CHIPS):
            for s in range(8):
                pair = part[chip, KV_ROWS + s * 16 : KV_ROWS + (s + 1) * 16, :].astype(F32)
                table.append(jnp.concatenate([pair[:8], pair[8:]], axis=1))
    table = jnp.concatenate(table, axis=0).astype(BF16)
    total = 512
    at = iota((total, 1), 0)
    sender_core = jnp.where(at >= 256, 1 - core, core)
    chip, s, to, slot = (at >> 6) & 3, (at >> 3) & 7, (at >> 2) & 1, at & 3
    sender = (
        (s >> 2) * 32 + (chip >> 1) * 16 + (s & 3) * 4 + (chip & 1) * 2 + sender_core
    )
    wide = iota((total, DOMS), 1)
    held = jnp.broadcast_to(counts[...].astype(F32), (8, DOMS)).astype(BF16)
    count = mm((sender == wide).astype(BF16), held, ((1,), (1,)))[:, 0:1]
    live_slot = (to == core) & (slot.astype(F32) < count)
    ids = jnp.where(live_slot, NODES + sender * SLOTS + slot, -1)
    ids = jnp.concatenate([iota((NODES, 1), 0), ids], axis=0)
    pick = (ids == src_row).astype(F32).astype(BF16)
    to_node = iota((NODES, 1), 0) == dst_row
    pick_dst = to_node.astype(F32).astype(BF16)
    hit = mm(jnp.ones((8, ids.shape[0]), BF16), pick)[0:1, :]
    live = jnp.where(iota((1, edges), 1) < limit[0], hit, 0.0)
    src_feats = mm(table, pick, ((0,), (0,))).astype(BF16)
    dst_feats = mm(normed[...], pick_dst, ((0,), (0,))).astype(BF16)
    column = lambda ref: jnp.broadcast_to(ref[...], (8, WIDTH)).T[:, 0:1]
    pre = (
        mm(w_src[...], src_feats, ((0,), (0,)))
        + mm(w_dst[...], dst_feats, ((0,), (0,)))
        + column(b1)
    )
    hidden = jax.nn.silu(pre).astype(BF16)
    message = (mm(w_out[...], hidden, ((0,), (0,))) + column(b2)).astype(BF16)
    spread = jnp.where(to_node, live, 0.0).astype(BF16)
    out[...] = feats[...] + mm(spread, message, ((1,), (1,)))


def finish_kernel(base, attended, w_out, gain, up, down, out):
    turned = jnp.concatenate([attended[h] for h in range(HEADS)], axis=0)
    mid = base[...] + mm(turned, w_out[...], ((0,), (0,)))
    lifted = jax.nn.gelu(mm(rms(mid, gain[...]).astype(BF16), up[...])).astype(BF16)
    out[...] = mid + mm(lifted, down[...])


def body(
    node_feats,
    norm_gain,
    w_query,
    w_key,
    w_value,
    w_out,
    msg_src_w,
    msg_dst_w,
    msg_bias,
    msg_out_w,
    msg_out_bias,
    mlp_gain,
    mlp_up,
    mlp_down,
    send_list,
    send_count,
    edge_src,
    edge_dst,
    edge_count,
):
    shape = pltpu.VMEM
    row = lambda v: v.reshape(1, WIDTH)
    vmem = lambda v: pltpu.with_memory_space_constraint(v, pltpu.VMEM)
    normed, sent = pl.pallas_call(
        project_kernel,
        out_shape=(shape((NODES, WIDTH), BF16), shape((HEADS, 160, 128), BF16)),
        in_specs=[VM] * 6,
        out_specs=(VM, VM),
        name="project",
    )(node_feats, row(norm_gain), w_query, w_key, w_value, jnp.swapaxes(send_list, 1, 2))
    got = lax.all_to_all(sent, HEAD_AXES, 0, 0, tiled=True)
    shared, own = pl.pallas_call(
        repack_kernel,
        out_shape=(shape((CHIPS, SENT_ROWS, 128), BF16), shape((8, KV, 128), BF16)),
        in_specs=[VM],
        out_specs=(VM, VM),
        compiler_params=ROOM,
        name="repack",
    )(vmem(got))
    mine = lax.all_to_all(shared, CHIP_AXES, 0, 0, tiled=True)
    partner = lax.ppermute(own, "core", [(0, 1), (1, 0)])
    other = lax.ppermute(mine, "core", [(0, 1), (1, 0)])
    place = (lax.axis_index("yb") * 2 + lax.axis_index("zb")).reshape(1).astype(jnp.int32)

    def attention(kernel, keys, out, *operands):
        scratch = [
            pltpu.VMEM((RING, HEAD), BF16),
            pltpu.VMEM((HEAD, keys), BF16),
            pltpu.VMEM((KV, keys), BF16),
        ]
        specs = [SM if v is place else VM for v in operands]
        return pl.pallas_call(
            kernel,
            out_shape=out,
            in_specs=specs,
            out_specs=VM,
            scratch_shapes=scratch,
            compiler_params=ROOM,
        )(*[v if v is place else vmem(v) for v in operands])

    state = shape((RING, KV), F32)
    held = attention(attend_own_kernel, 2 * RING, state, got, partner)
    held = attention(attend_near_kernel, 3 * RING, state, place, got, mine, held)
    attended = attention(
        attend_last_kernel, 3 * RING, shape((8, HEAD, NODES), BF16), place, got, other, held
    )
    back = lax.all_to_all(attended, HEAD_AXES, 0, 0, tiled=True)
    core = lax.axis_index("core").reshape(1).astype(jnp.int32)
    base = pl.pallas_call(
        edge_kernel,
        out_shape=shape((NODES, WIDTH), F32),
        in_specs=[SM, SM] + [VM] * 12,
        out_specs=VM,
        compiler_params=ROOM,
        name="edges",
    )(
        edge_count,
        core,
        vmem(normed),
        vmem(mine),
        vmem(other),
        send_count.T,
        edge_src,
        edge_dst,
        vmem(msg_src_w),
        vmem(msg_dst_w),
        row(msg_bias),
        vmem(msg_out_w),
        row(msg_out_bias),
        node_feats,
    )
    return pl.pallas_call(
        finish_kernel,
        out_shape=jax.ShapeDtypeStruct((NODES, WIDTH), F32),
        in_specs=[VM] * 6,
        out_specs=VM,
        compiler_params=ROOM,
        name="finish",
    )(vmem(base), vmem(back), vmem(w_out), row(mlp_gain), vmem(mlp_up), vmem(mlp_down))


def solution(mesh):
    finer = Mesh(
        mesh.devices.reshape(mesh.shape["graphs"], 2, 2, 4, 2, 2), ("graphs",) + DOM
    )
    rows = P(GRAPHS_DOM, None)
    blocks = P(GRAPHS_DOM, None, None)
    placed = (rows,) + (P(),) * 13 + (blocks, P("graphs", DOM), blocks, blocks, P(GRAPHS_DOM))

    return jax.shard_map(body, mesh=finer, in_specs=placed, out_specs=rows, check_vma=False)
```

```python
import math

import jax
import jax.numpy as jnp
from jax import lax
from jax.experimental import pallas as pl
from jax.experimental.pallas import tpu as pltpu
from jax.sharding import Mesh
from jax.sharding import PartitionSpec as P


HEADS = 8
NODES = 128
WIDTH = 256
HEAD = WIDTH // HEADS
SLOTS = 4
DOMS = 64
DOM = ("ya", "yb", "za", "zb", "core")
GRAPHS_DOM = ("graphs",) + DOM
CHIP_AXES = ("yb", "zb")
CHIPS = 4
FIRST = 3


def block_of(j):
    return (j >> 2) * 32 + ((j + FIRST) & 3) * 4


def zb_of(j, group):
    return group ^ (((j + FIRST) & 3) >> 1)


HEAD_GROUPS = [
    [block_of(j) + yb * 16 + zb_of(j, group) * 2 + core for j in range(8)]
    for yb in range(2)
    for group in range(2)
    for core in range(2)
]
F32 = jnp.float32
BF16 = jnp.bfloat16
SCALE = math.log2(math.e) / math.sqrt(HEAD)
VM = pl.BlockSpec(memory_space=pltpu.VMEM)
SM = pl.BlockSpec(memory_space=pltpu.SMEM)
KV = 2 * HEAD
KV_ROWS = 8 * KV
SENT_ROWS = KV_ROWS + 8 * 16
RING = 8 * NODES
Q_BLOCK = 256
TOP_LANE = 48
ROOM = pltpu.CompilerParams(vmem_limit_bytes=28 * 2**20)


def iota(shape, dim):
    return lax.broadcasted_iota(jnp.int32, shape, dim)


def mm(a, b, dims=((1,), (0,))):
    return lax.dot_general(a, b, (dims, ((), ())), preferred_element_type=F32)


def rms(x, gain):
    return x * lax.rsqrt(jnp.mean(x * x, axis=-1, keepdims=True) + 1e-06) * gain


def project_kernel(feats, gain, wq, wk, wv, lists, normed_out, sent):
    normed = rms(feats[...], gain[...]).astype(BF16)
    normed_out[...] = normed
    for first, weight, factor in ((0, wq, SCALE), (HEAD, wk, None), (2 * HEAD, wv, None)):
        out = mm(normed, weight[...])
        if factor is not None:
            out = out * factor
        turned = out.T.astype(BF16)
        for h in range(HEADS):
            sent[h, first : first + HEAD, :] = turned[h * HEAD : (h + 1) * HEAD, :]
    place = iota((DOMS * SLOTS, DOMS), 0)
    receiver = (
        block_of(place >> 5)
        + ((place >> 4) & 1) * 16
        + ((place >> 2) & 3)
    )
    pick_receiver = (receiver == iota((DOMS * SLOTS, DOMS), 1)).astype(BF16)
    spread = mm(pick_receiver, lists[0].astype(F32).astype(BF16), ((1,), (1,)))
    own_slot = (iota(spread.shape, 0) & 3) == iota(spread.shape, 1)
    index = jnp.sum(jnp.where(own_slot, spread, 0.0), axis=1, keepdims=True)
    lanes = iota((DOMS * SLOTS, NODES), 1).astype(F32)
    rows = mm((lanes == index).astype(BF16), normed)
    for h in range(HEADS):
        parts = []
        for chip in range(CHIPS):
            at = h * 32 + chip * 8
            parts += [rows[at : at + 8, :128], rows[at : at + 8, 128:]]
        sent[h, 3 * HEAD :, :] = jnp.concatenate(parts, axis=0).astype(BF16)


def repack_kernel(got, sent, own):
    for s in range(8):
        own[s] = got[s, HEAD : 3 * HEAD, :]
    for chip in range(CHIPS):
        for s in range(8):
            sent[chip, s * 64 : (s + 1) * 64, :] = got[s, HEAD : 3 * HEAD, :]
            sent[chip, KV_ROWS + s * 16 : KV_ROWS + (s + 1) * 16, :] = got[
                s, 96 + chip * 16 : 112 + chip * 16, :
            ]


def load_queries(got, q_s):
    for s in range(8):
        q_s[s * 128 : (s + 1) * 128, :] = got[s, 0:HEAD, :].T


def load_keys(pieces, k_s, v_s):
    for at, piece in enumerate(pieces):
        lanes = slice(at * 128, (at + 1) * 128)
        k_s[:, lanes] = piece[:HEAD, :]
        v_s[0:HEAD, lanes] = piece[HEAD:, :]
    v_s[HEAD:, :] = jnp.ones((HEAD, v_s.shape[1]), BF16)


def attend(q_s, k_s, v_s, before, after):
    def scores_of(b):
        return mm(q_s[b * Q_BLOCK : (b + 1) * Q_BLOCK, :], k_s[...])

    blocks = RING // Q_BLOCK
    scores = scores_of(0)
    for b in range(blocks):
        upcoming = scores_of(b + 1) if b + 1 < blocks else None
        at = slice(b * Q_BLOCK, (b + 1) * Q_BLOCK)
        top = jnp.max(scores, axis=1, keepdims=True)
        if before is not None:
            old = before[at, TOP_LANE : TOP_LANE + 1]
            top = jnp.maximum(old, top)
        weights = jnp.exp2(scores - top).astype(BF16)
        acc = mm(weights, v_s[...], ((1,), (1,)))
        if before is not None:
            acc = acc + before[at, :] * jnp.exp2(old - top)
        after(b, at, acc, top)
        scores = upcoming


def keep(state_out):
    def after(b, at, acc, top):
        state_out[at, :] = jnp.where(iota(acc.shape, 1) < TOP_LANE, acc, top)

    return after


def attend_own_kernel(got, partner, state, q_s, k_s, v_s):
    load_queries(got, q_s)
    pieces = [got[s, HEAD : 3 * HEAD, :] for s in range(8)]
    load_keys(pieces + [partner[s] for s in range(8)], k_s, v_s)
    attend(q_s, k_s, v_s, None, keep(state))


def load_near(place, got, kv, q_s, k_s, v_s):
    load_queries(got, q_s)
    pieces = []
    for turn in range(1, CHIPS):
        chip = (place[0] + turn) & (CHIPS - 1)
        pieces += [kv[chip, s * KV : (s + 1) * KV, :] for s in range(8)]
    load_keys(pieces, k_s, v_s)


def attend_near_kernel(place, got, kv, before, state, q_s, k_s, v_s):
    load_near(place, got, kv, q_s, k_s, v_s)
    attend(q_s, k_s, v_s, before, keep(state))


def attend_last_kernel(place, got, kv, before, out, q_s, k_s, v_s):
    load_near(place, got, kv, q_s, k_s, v_s)

    def after(b, at, acc, top):
        done = (acc[:, :HEAD] / acc[:, HEAD : HEAD + 1]).T.astype(BF16)
        for i in range(Q_BLOCK // 128):
            out[b * (Q_BLOCK // 128) + i] = done[:, i * 128 : (i + 1) * 128]

    attend(q_s, k_s, v_s, before, after)


def edge_kernel(
    limit, place, normed, mine, other, counts, src, dst, w_src, w_dst, b1, w_out, b2, feats, out
):
    edges = src.shape[1] * src.shape[2]
    tiles = src.shape[1]
    row = lambda ref: jnp.concatenate([ref[0, t : t + 1, :] for t in range(tiles)], axis=1)
    src_row, dst_row = row(src), row(dst)
    core, far = place[0], place[1]
    table = [normed[...].astype(F32)]
    for part in (mine, other):
        for chip in range(CHIPS):
            for s in range(8):
                pair = part[chip, KV_ROWS + s * 16 : KV_ROWS + (s + 1) * 16, :].astype(F32)
                table.append(jnp.concatenate([pair[:8], pair[8:]], axis=1))
    table = jnp.concatenate(table, axis=0).astype(BF16)
    total = 512
    at = iota((total, 1), 0)
    sender_core = jnp.where(at >= 256, 1 - core, core)
    chip, s, to, slot = (at >> 6) & 3, (at >> 3) & 7, (at >> 2) & 1, at & 3
    group = (chip & 1) ^ far
    sender = block_of(s) + (chip >> 1) * 16 + zb_of(s, group) * 2 + sender_core
    wide = iota((total, DOMS), 1)
    held = jnp.broadcast_to(counts[...].astype(F32), (8, DOMS)).astype(BF16)
    count = mm((sender == wide).astype(BF16), held, ((1,), (1,)))[:, 0:1]
    live_slot = (to == core) & (slot.astype(F32) < count)
    ids = jnp.where(live_slot, NODES + sender * SLOTS + slot, -1)
    ids = jnp.concatenate([iota((NODES, 1), 0), ids], axis=0)
    pick = (ids == src_row).astype(F32).astype(BF16)
    to_node = iota((NODES, 1), 0) == dst_row
    pick_dst = to_node.astype(F32).astype(BF16)
    hit = mm(jnp.ones((8, ids.shape[0]), BF16), pick)[0:1, :]
    live = jnp.where(iota((1, edges), 1) < limit[0], hit, 0.0)
    src_feats = mm(table, pick, ((0,), (0,))).astype(BF16)
    dst_feats = mm(normed[...], pick_dst, ((0,), (0,))).astype(BF16)
    column = lambda ref: jnp.broadcast_to(ref[...], (8, WIDTH)).T[:, 0:1]
    pre = (
        mm(w_src[...], src_feats, ((0,), (0,)))
        + mm(w_dst[...], dst_feats, ((0,), (0,)))
        + column(b1)
    )
    hidden = jax.nn.silu(pre).astype(BF16)
    message = (mm(w_out[...], hidden, ((0,), (0,))) + column(b2)).astype(BF16)
    spread = jnp.where(to_node, live, 0.0).astype(BF16)
    out[...] = feats[...] + mm(spread, message, ((1,), (1,)))


def finish_kernel(base, attended, w_out, gain, up, down, out):
    turned = jnp.concatenate([attended[h] for h in range(HEADS)], axis=0)
    mid = base[...] + mm(turned, w_out[...], ((0,), (0,)))
    lifted = jax.nn.gelu(mm(rms(mid, gain[...]).astype(BF16), up[...])).astype(BF16)
    out[...] = mid + mm(lifted, down[...])


def body(
    node_feats,
    norm_gain,
    w_query,
    w_key,
    w_value,
    w_out,
    msg_src_w,
    msg_dst_w,
    msg_bias,
    msg_out_w,
    msg_out_bias,
    mlp_gain,
    mlp_up,
    mlp_down,
    send_list,
    send_count,
    edge_src,
    edge_dst,
    edge_count,
):
    shape = pltpu.VMEM
    row = lambda v: v.reshape(1, WIDTH)
    vmem = lambda v: pltpu.with_memory_space_constraint(v, pltpu.VMEM)
    normed, sent = pl.pallas_call(
        project_kernel,
        out_shape=(shape((NODES, WIDTH), BF16), shape((HEADS, 160, 128), BF16)),
        in_specs=[VM] * 6,
        out_specs=(VM, VM),
        name="project",
    )(node_feats, row(norm_gain), w_query, w_key, w_value, jnp.swapaxes(send_list, 1, 2))
    got = lax.all_to_all(
        sent, DOM, 0, 0, axis_index_groups=HEAD_GROUPS, tiled=True
    )
    shared, own = pl.pallas_call(
        repack_kernel,
        out_shape=(shape((CHIPS, SENT_ROWS, 128), BF16), shape((8, KV, 128), BF16)),
        in_specs=[VM],
        out_specs=(VM, VM),
        compiler_params=ROOM,
        name="repack",
    )(vmem(got))
    mine = lax.all_to_all(shared, CHIP_AXES, 0, 0, tiled=True)
    partner = lax.ppermute(own, "core", [(0, 1), (1, 0)])
    other = lax.ppermute(mine, "core", [(0, 1), (1, 0)])
    place = (lax.axis_index("yb") * 2 + lax.axis_index("zb")).reshape(1).astype(jnp.int32)

    def attention(kernel, keys, out, *operands):
        scratch = [
            pltpu.VMEM((RING, HEAD), BF16),
            pltpu.VMEM((HEAD, keys), BF16),
            pltpu.VMEM((KV, keys), BF16),
        ]
        specs = [SM if v is place else VM for v in operands]
        return pl.pallas_call(
            kernel,
            out_shape=out,
            in_specs=specs,
            out_specs=VM,
            scratch_shapes=scratch,
            compiler_params=ROOM,
        )(*[v if v is place else vmem(v) for v in operands])

    state = shape((RING, KV), F32)
    held = attention(attend_own_kernel, 2 * RING, state, got, partner)
    held = attention(attend_near_kernel, 3 * RING, state, place, got, mine, held)
    attended = attention(
        attend_last_kernel, 3 * RING, shape((8, HEAD, NODES), BF16), place, got, other, held
    )
    back = lax.all_to_all(
        attended, DOM, 0, 0, axis_index_groups=HEAD_GROUPS, tiled=True
    )
    core = jnp.stack([lax.axis_index("core"), lax.axis_index("za") >> 1]).astype(jnp.int32)
    base = pl.pallas_call(
        edge_kernel,
        out_shape=shape((NODES, WIDTH), F32),
        in_specs=[SM, SM] + [VM] * 12,
        out_specs=VM,
        compiler_params=ROOM,
        name="edges",
    )(
        edge_count,
        core,
        vmem(normed),
        vmem(mine),
        vmem(other),
        send_count.T,
        edge_src,
        edge_dst,
        vmem(msg_src_w),
        vmem(msg_dst_w),
        row(msg_bias),
        vmem(msg_out_w),
        row(msg_out_bias),
        node_feats,
    )
    return pl.pallas_call(
        finish_kernel,
        out_shape=jax.ShapeDtypeStruct((NODES, WIDTH), F32),
        in_specs=[VM] * 6,
        out_specs=VM,
        compiler_params=ROOM,
        name="finish",
    )(vmem(base), vmem(back), vmem(w_out), row(mlp_gain), vmem(mlp_up), vmem(mlp_down))


def solution(mesh):
    finer = Mesh(
        mesh.devices.reshape(mesh.shape["graphs"], 2, 2, 4, 2, 2), ("graphs",) + DOM
    )
    rows = P(GRAPHS_DOM, None)
    blocks = P(GRAPHS_DOM, None, None)
    placed = (rows,) + (P(),) * 13 + (blocks, P("graphs", DOM), blocks, blocks, P(GRAPHS_DOM))

    return jax.shard_map(body, mesh=finer, in_specs=placed, out_specs=rows, check_vma=False)
```

```python
import math

import jax
import jax.numpy as jnp
from jax import lax
from jax.experimental import pallas as pl
from jax.experimental.pallas import tpu as pltpu
from jax.sharding import Mesh
from jax.sharding import PartitionSpec as P


HEADS = 8
NODES = 128
WIDTH = 256
HEAD = WIDTH // HEADS
SLOTS = 4
DOMS = 64
DOM = ("ya", "yb", "za", "zb", "core")
GRAPHS_DOM = ("graphs",) + DOM
CHIP_AXES = ("yb", "zb")
CHIPS = 4
FIRST = 2


def block_of(j):
    return (j >> 2) * 32 + ((j + FIRST) & 3) * 4


def zb_of(j, group):
    return group ^ (((j + FIRST) & 3) >> 1)


HEAD_GROUPS = [
    [block_of(j) + yb * 16 + zb_of(j, group) * 2 + core for j in range(8)]
    for yb in range(2)
    for group in range(2)
    for core in range(2)
]
F32 = jnp.float32
BF16 = jnp.bfloat16
SCALE = math.log2(math.e) / math.sqrt(HEAD)
VM = pl.BlockSpec(memory_space=pltpu.VMEM)
SM = pl.BlockSpec(memory_space=pltpu.SMEM)
ANY = pl.BlockSpec(memory_space=pl.ANY)
KV = 2 * HEAD
RING = 8 * NODES
Q_BLOCK = 256
TOP_LANE = 48
ROOM = pltpu.CompilerParams(vmem_limit_bytes=28 * 2**20)


def iota(shape, dim):
    return lax.broadcasted_iota(jnp.int32, shape, dim)


def mm(a, b, dims=((1,), (0,))):
    return lax.dot_general(a, b, (dims, ((), ())), preferred_element_type=F32)


def rms(x, gain):
    return x * lax.rsqrt(jnp.mean(x * x, axis=-1, keepdims=True) + 1e-06) * gain


def project_kernel(feats, gain, wq, wk, wv, lists, normed_out, sent):
    normed = rms(feats[...], gain[...]).astype(BF16)
    normed_out[...] = normed
    for first, weight, factor in ((0, wq, SCALE), (HEAD, wk, None), (2 * HEAD, wv, None)):
        out = mm(normed, weight[...])
        if factor is not None:
            out = out * factor
        turned = out.T.astype(BF16)
        for h in range(HEADS):
            sent[h, first : first + HEAD, :] = turned[h * HEAD : (h + 1) * HEAD, :]
    place = iota((DOMS * SLOTS, DOMS), 0)
    receiver = (
        block_of(place >> 5)
        + ((place >> 4) & 1) * 16
        + ((place >> 2) & 3)
    )
    pick_receiver = (receiver == iota((DOMS * SLOTS, DOMS), 1)).astype(BF16)
    spread = mm(pick_receiver, lists[0].astype(F32).astype(BF16), ((1,), (1,)))
    own_slot = (iota(spread.shape, 0) & 3) == iota(spread.shape, 1)
    index = jnp.sum(jnp.where(own_slot, spread, 0.0), axis=1, keepdims=True)
    lanes = iota((DOMS * SLOTS, NODES), 1).astype(F32)
    rows = mm((lanes == index).astype(BF16), normed)
    for h in range(HEADS):
        parts = []
        for chip in range(CHIPS):
            at = h * 32 + chip * 8
            parts += [rows[at : at + 8, :128], rows[at : at + 8, 128:]]
        sent[h, 3 * HEAD :, :] = jnp.concatenate(parts, axis=0).astype(BF16)


def repack_kernel(got, sent, own, done):
    keys = got.at[:, HEAD : 3 * HEAD, :]
    copies = [pltpu.make_async_copy(keys, own, done.at[0])]
    for chip in range(CHIPS):
        rows = got.at[:, 96 + chip * 16 : 112 + chip * 16, :]
        copies += [
            pltpu.make_async_copy(keys, sent.at[chip, :, :KV, :], done.at[1 + 2 * chip]),
            pltpu.make_async_copy(rows, sent.at[chip, :, KV:, :], done.at[2 + 2 * chip]),
        ]
    for copy in copies:
        copy.start()
    for copy in copies:
        copy.wait()


def load_queries(got, q_s):
    for s in range(8):
        q_s[s * 128 : (s + 1) * 128, :] = got[s, 0:HEAD, :].T


def load_keys(pieces, k_s, v_s):
    for at, piece in enumerate(pieces):
        lanes = slice(at * 128, (at + 1) * 128)
        k_s[:, lanes] = piece[:HEAD, :]
        v_s[0:HEAD, lanes] = piece[HEAD:, :]
    v_s[HEAD:, :] = jnp.ones((HEAD, v_s.shape[1]), BF16)


def attend(q_s, k_s, v_s, before, after):
    def scores_of(b):
        return mm(q_s[b * Q_BLOCK : (b + 1) * Q_BLOCK, :], k_s[...])

    blocks = RING // Q_BLOCK
    scores = scores_of(0)
    for b in range(blocks):
        upcoming = scores_of(b + 1) if b + 1 < blocks else None
        at = slice(b * Q_BLOCK, (b + 1) * Q_BLOCK)
        top = jnp.max(scores, axis=1, keepdims=True)
        if before is not None:
            old = before[at, TOP_LANE : TOP_LANE + 1]
            top = jnp.maximum(old, top)
        weights = jnp.exp2(scores - top).astype(BF16)
        acc = mm(weights, v_s[...], ((1,), (1,)))
        if before is not None:
            acc = acc + before[at, :] * jnp.exp2(old - top)
        after(b, at, acc, top)
        scores = upcoming


def keep(state_out):
    def after(b, at, acc, top):
        state_out[at, :] = jnp.where(iota(acc.shape, 1) < TOP_LANE, acc, top)

    return after


def attend_own_kernel(got, partner, state, q_s, k_s, v_s):
    load_queries(got, q_s)
    pieces = [got[s, HEAD : 3 * HEAD, :] for s in range(8)]
    load_keys(pieces + [partner[s] for s in range(8)], k_s, v_s)
    attend(q_s, k_s, v_s, None, keep(state))


def load_near(place, kv, k_s, v_s):
    pieces = []
    for turn in range(1, CHIPS):
        chip = (place[0] + turn) & (CHIPS - 1)
        pieces += [kv[chip, s, :KV, :] for s in range(8)]
    load_keys(pieces, k_s, v_s)


def attend_near_kernel(place, q_s, kv, before, state, k_s, v_s):
    load_near(place, kv, k_s, v_s)
    attend(q_s, k_s, v_s, before, keep(state))


def attend_last_kernel(place, q_s, kv, before, out, k_s, v_s):
    load_near(place, kv, k_s, v_s)

    def after(b, at, acc, top):
        turned = acc.T
        done = (turned[:HEAD, :] / turned[HEAD : HEAD + 1, :]).astype(BF16)
        for i in range(Q_BLOCK // 128):
            out[b * (Q_BLOCK // 128) + i] = done[:, i * 128 : (i + 1) * 128]

    attend(q_s, k_s, v_s, before, after)


def edge_match_kernel(place, limit, counts, src, ids_out, live_out):
    edges = src.shape[1] * src.shape[2]
    tiles = src.shape[1]
    row = lambda ref: jnp.concatenate([ref[0, t : t + 1, :] for t in range(tiles)], axis=1)
    src_row = row(src)
    core, far = place[0], place[1]
    total = 512
    at = iota((total, 1), 0)
    sender_core = jnp.where(at >= 256, 1 - core, core)
    chip, s, to, slot = (at >> 6) & 3, (at >> 3) & 7, (at >> 2) & 1, at & 3
    group = (chip & 1) ^ far
    sender = block_of(s) + (chip >> 1) * 16 + zb_of(s, group) * 2 + sender_core
    wide = iota((total, DOMS), 1)
    held = jnp.broadcast_to(counts[...].astype(F32), (8, DOMS)).astype(BF16)
    count = mm((sender == wide).astype(BF16), held, ((1,), (1,)))[:, 0:1]
    live_slot = (to == core) & (slot.astype(F32) < count)
    ids = jnp.where(live_slot, NODES + sender * SLOTS + slot, -1)
    ids = jnp.concatenate([iota((NODES, 1), 0), ids], axis=0)
    pick = (ids == src_row).astype(F32).astype(BF16)
    ids_out[...] = ids
    hit = mm(jnp.ones((8, ids.shape[0]), BF16), pick)[0:1, :]
    live_out[...] = jnp.where(iota((1, edges), 1) < limit[...], hit, 0.0)


def edge_kernel(
    normed, mine, other, ids, live, src, dst, w_src, w_dst, b1, w_out, b2, feats, out
):
    tiles = src.shape[1]
    row = lambda ref: jnp.concatenate([ref[0, t : t + 1, :] for t in range(tiles)], axis=1)
    src_row, dst_row = row(src), row(dst)
    table = [normed[...].astype(F32)]
    for part in (mine, other):
        for chip in range(CHIPS):
            for s in range(8):
                pair = part[chip, s, KV:, :].astype(F32)
                table.append(jnp.concatenate([pair[:8], pair[8:]], axis=1))
    table = jnp.concatenate(table, axis=0).astype(BF16)
    pick = (ids[...] == src_row).astype(F32).astype(BF16)
    to_node = iota((NODES, 1), 0) == dst_row
    pick_dst = to_node.astype(F32).astype(BF16)
    src_feats = mm(table, pick, ((0,), (0,))).astype(BF16)
    dst_feats = mm(normed[...], pick_dst, ((0,), (0,))).astype(BF16)
    column = lambda ref: jnp.broadcast_to(ref[...], (8, WIDTH)).T[:, 0:1]
    pre = (
        mm(w_src[...], src_feats, ((0,), (0,)))
        + mm(w_dst[...], dst_feats, ((0,), (0,)))
        + column(b1)
    )
    hidden = jax.nn.silu(pre).astype(BF16)
    message = (mm(w_out[...], hidden, ((0,), (0,))) + column(b2)).astype(BF16)
    out[...] = feats[...] + mm(jnp.where(to_node, live[...], 0.0).astype(BF16), message, ((1,), (1,)))


def finish_kernel(base, attended, w_out, gain, up, down, out):
    turned = jnp.concatenate([attended[h] for h in range(HEADS)], axis=0)
    mid = base[...] + mm(turned, w_out[...], ((0,), (0,)))
    lifted = jax.nn.gelu(mm(rms(mid, gain[...]).astype(BF16), up[...])).astype(BF16)
    out[...] = mid + mm(lifted, down[...])


def body(
    node_feats,
    norm_gain,
    w_query,
    w_key,
    w_value,
    w_out,
    msg_src_w,
    msg_dst_w,
    msg_bias,
    msg_out_w,
    msg_out_bias,
    mlp_gain,
    mlp_up,
    mlp_down,
    send_list,
    send_count,
    edge_src,
    edge_dst,
    edge_count,
):
    shape = pltpu.VMEM
    row = lambda v: v.reshape(1, WIDTH)
    vmem = lambda v: pltpu.with_memory_space_constraint(v, pltpu.VMEM)
    normed, sent = pl.pallas_call(
        project_kernel,
        out_shape=(shape((NODES, WIDTH), BF16), shape((HEADS, 160, 128), BF16)),
        in_specs=[VM] * 6,
        out_specs=(VM, VM),
        name="project",
    )(node_feats, row(norm_gain), w_query, w_key, w_value, jnp.swapaxes(send_list, 1, 2))
    got = lax.all_to_all(
        sent, DOM, 0, 0, axis_index_groups=HEAD_GROUPS, tiled=True
    )
    shared, own = pl.pallas_call(
        repack_kernel,
        out_shape=(jax.ShapeDtypeStruct((CHIPS, 8, KV + 16, 128), BF16), shape((8, KV, 128), BF16)),
        in_specs=[VM],
        out_specs=(ANY, VM),
        scratch_shapes=[pltpu.SemaphoreType.DMA((1 + 2 * CHIPS,))],
        compiler_params=ROOM,
        name="repack",
    )(vmem(got))
    mine = lax.all_to_all(shared, CHIP_AXES, 0, 0, tiled=True)
    partner = lax.ppermute(own, "core", [(0, 1), (1, 0)])
    other = lax.ppermute(mine, "core", [(0, 1), (1, 0)])
    place = (lax.axis_index("yb") * 2 + lax.axis_index("zb")).reshape(1).astype(jnp.int32)

    def attention(kernel, keys, out, *operands):
        scratch = [
            pltpu.VMEM((HEAD, keys), BF16),
            pltpu.VMEM((KV, keys), BF16),
        ]
        specs = [SM if v is place else VM for v in operands]
        return pl.pallas_call(
            kernel,
            out_shape=out,
            in_specs=specs,
            out_specs=(VM, VM) if isinstance(out, tuple) else VM,
            scratch_shapes=scratch,
            compiler_params=ROOM,
        )(*[v if v is place else vmem(v) for v in operands])

    state = shape((RING, KV), F32)
    turned = shape((RING, HEAD), BF16)
    held, queries = attention(attend_own_kernel, 2 * RING, (state, turned), got, partner)
    held = attention(attend_near_kernel, 3 * RING, state, place, queries, mine, held)
    attended = attention(
        attend_last_kernel, 3 * RING, shape((8, HEAD, NODES), BF16), place, queries, other, held
    )
    back = lax.all_to_all(
        attended, DOM, 0, 0, axis_index_groups=HEAD_GROUPS, tiled=True
    )
    core = jnp.stack([lax.axis_index("core"), lax.axis_index("za") >> 1]).astype(jnp.int32)
    edges = edge_src.shape[1] * edge_src.shape[2]
    ids, live = pl.pallas_call(
        edge_match_kernel,
        out_shape=(shape((NODES + 512, 1), jnp.int32), shape((1, edges), F32)),
        in_specs=[SM] + [VM] * 3,
        out_specs=(VM, VM),
        compiler_params=ROOM,
        name="edge_match",
    )(core, edge_count.reshape(1, 1), send_count.T, edge_src)
    base = pl.pallas_call(
        edge_kernel,
        out_shape=shape((NODES, WIDTH), F32),
        in_specs=[VM] * 13,
        out_specs=VM,
        compiler_params=ROOM,
        name="edges",
    )(
        vmem(normed),
        vmem(mine),
        vmem(other),
        vmem(ids),
        vmem(live),
        vmem(edge_src),
        vmem(edge_dst),
        vmem(msg_src_w),
        vmem(msg_dst_w),
        row(msg_bias),
        vmem(msg_out_w),
        row(msg_out_bias),
        node_feats,
    )
    return pl.pallas_call(
        finish_kernel,
        out_shape=jax.ShapeDtypeStruct((NODES, WIDTH), F32),
        in_specs=[VM] * 6,
        out_specs=VM,
        compiler_params=ROOM,
        name="finish",
    )(vmem(base), vmem(back), vmem(w_out), row(mlp_gain), vmem(mlp_up), vmem(mlp_down))


def solution(mesh):
    finer = Mesh(
        mesh.devices.reshape(mesh.shape["graphs"], 2, 2, 4, 2, 2), ("graphs",) + DOM
    )
    rows = P(GRAPHS_DOM, None)
    blocks = P(GRAPHS_DOM, None, None)
    placed = (rows,) + (P(),) * 13 + (blocks, P("graphs", DOM), blocks, blocks, P(GRAPHS_DOM))

    return jax.shard_map(body, mesh=finer, in_specs=placed, out_specs=rows, check_vma=False)
```
